32 devices in a mesh: grp: 2 (over x), seq: 16 (over z, y, core).
Axes of the slice: x: 2, y: 2, z: 4, core: 2. Of those that a mesh axis runs over, the one named last changes fastest.
Arguments:
- query_vectors: bfloat16 [4096, 4096], P(('grp', 'seq')), parts along dimension 0, may hold values from -0.5 to 0.5
- key_vectors: bfloat16 [4096, 4096], P(('grp', 'seq')), parts along dimension 0, may hold values from -0.5 to 0.5
- value_vectors: bfloat16 [4096, 2048], P(('grp', 'seq')), parts along dimension 0, may hold values from -6 to 6
- level_weights: bfloat16 [12, 32, 4096], P(None, None, ('grp', 'seq')), parts along dimension 2, may hold values from 0.049804688 to 0.5
Outputs:
- attended: bfloat16 [4096, 2048], P(('grp', 'seq')), parts along dimension 0
The draws below stay inside these ranges and needn't reach their ends.
There are 2 independent parts, one for each index of `grp`. The reference program is written for one: setup_inputs(seed, part) draws one part's arguments, and reference() takes and returns one part's arrays. A program takes and returns all parts, laid end to end along the dimension named above; each array names one. Nothing has to cross between parts.
All inputs are finite; a program needn't handle non-finite values.
Results may differ from the reference program's by a relative error of at most 0.0019.
Values sent between devices are 32-bit elements; how exact they have to be, the bound alone decides.
A program may use at most 64 MiB of HBM per device.

```python
import math
import jax
import jax.numpy as jnp
from jax import lax

HEADS = 32
STATE = 128
HEAD_DIM = 64
TOK_DEV = 128
TOKENS = 2048
LEVELS = 12
N_SEQ = 16


def shard_levels(own_key, dims, cuts, least, high):
    def one(position, parts):
        steps = jax.random.uniform(jax.random.fold_in(jax.random.fold_in(own_key, 6), position), (parts,), jnp.float32, least / len(cuts), high / len(cuts))
        return jnp.repeat(jnp.exp(steps), dims[position] // parts).reshape((-1,) + (1,) * (len(dims) - position - 1))

    gain = one(*cuts[0])
    for cut in cuts[1:]:
        gain = gain * one(*cut)
    return gain


def scatter_about(key, shape, spread, reach, pieces=(), kind=jnp.bfloat16):
    values = spread * jax.random.normal(key, shape, jnp.float32)
    if pieces:
        values = values * shard_levels(key, shape, pieces, -0.22, 0.18)
    return jnp.clip(values, -reach, reach).astype(kind)


def setup_inputs(seed: int = 0, part: int = 0) -> dict:
    seeds = jax.random.split(jax.random.key(seed), 5)
    part_keys = jax.random.split(jax.random.fold_in(seeds[4], part), 5)
    query_vectors = scatter_about(part_keys[0], (TOKENS, HEADS * STATE), STATE ** -0.5, 0.5, ((0, 16),))
    key_vectors = scatter_about(part_keys[1], (TOKENS, HEADS * STATE), STATE ** -0.5, 0.5, ((0, 16),))
    value_vectors = scatter_about(part_keys[2], (TOKENS, HEADS * HEAD_DIM), 1.0, 6.0, ((0, 16),))
    level_weights = jnp.clip(jnp.exp(math.log(0.5) - 2.306499 * jax.random.uniform(part_keys[3], (LEVELS, HEADS, TOKENS), jnp.float32) ** shard_levels(part_keys[3], (LEVELS, HEADS, TOKENS), ((2, 16),), -0.2, 0.2)), 0.049804688, 0.5).astype(jnp.bfloat16)
    return {"query_vectors": query_vectors, "key_vectors": key_vectors, "value_vectors": value_vectors, "level_weights": level_weights}


def depth_table(block_size):
    query_pos = lax.broadcasted_iota(jnp.int32, (block_size, block_size), 0)
    key_pos = lax.broadcasted_iota(jnp.int32, (block_size, block_size), 1)
    depth_map = jnp.zeros((block_size, block_size), jnp.int32)
    for shift_bits in range(block_size.bit_length() - 1):
        differs = jnp.right_shift(query_pos, shift_bits) != jnp.right_shift(key_pos, shift_bits)
        depth_map = depth_map + differs.astype(jnp.int32)
    return depth_map, key_pos <= query_pos


def reference(query_vectors, key_vectors, value_vectors, level_weights):
    block_size = TOK_DEV
    blocks_count = N_SEQ
    local_levels = block_size.bit_length()
    seq_bits = blocks_count.bit_length() - 1
    highest = lax.Precision.HIGHEST
    queries = query_vectors.astype(jnp.float32).reshape(blocks_count, block_size, HEADS, STATE)
    keys_all = key_vectors.astype(jnp.float32).reshape(blocks_count, block_size, HEADS, STATE)
    values_all = value_vectors.astype(jnp.float32).reshape(blocks_count, block_size, HEADS, HEAD_DIM)
    weights_all = level_weights.astype(jnp.float32).reshape(LEVELS, HEADS, blocks_count, block_size).transpose(2, 0, 1, 3)
    depth_map, causal = depth_table(block_size)
    states = jnp.einsum("btgn,btgp->bgnp", keys_all, values_all, precision=highest)
    owner_ids = jnp.arange(blocks_count, dtype=jnp.int32)
    level_states = []
    for bit_index in range(seq_bits):
        span_size = 2 ** bit_index
        grouped = states.reshape(blocks_count // span_size, span_size, HEADS, STATE, HEAD_DIM).sum(axis=1)
        source = jnp.maximum(jnp.right_shift(owner_ids, bit_index) - 1, 0).astype(jnp.int32)
        upper_half = jnp.right_shift(owner_ids, bit_index) % 2 == 1
        picked = jnp.take(grouped, source, axis=0)
        level_states.append(jnp.where(upper_half[:, None, None, None], picked, 0.0))
    stacked = jnp.stack(level_states, axis=1)

    def one_block(operands):
        queries_b, keys_b, values_b, weights_b, states_b = operands
        scores = jnp.einsum("tgn,sgn->gts", queries_b, keys_b, precision=highest)
        lam_local = weights_b[:local_levels].transpose(1, 2, 0)
        index_map = jnp.broadcast_to(depth_map[None], (HEADS, block_size, block_size))
        mixing = jnp.take_along_axis(lam_local, index_map, axis=2)
        rounded = jnp.where(causal[None], mixing * scores, 0.0).astype(jnp.bfloat16)
        mixed = lax.optimization_barrier(rounded).astype(jnp.float32)
        local_term = jnp.einsum("gts,sgp->tgp", mixed, values_b, precision=highest)
        cross_term = jnp.zeros((block_size, HEADS, HEAD_DIM), jnp.float32)
        for bit_index in range(seq_bits):
            lam_row = weights_b[local_levels + bit_index].T
            product = jnp.einsum("thn,hnp->thp", queries_b, states_b[bit_index], precision=highest)
            cross_term = cross_term + lam_row[:, :, None] * product
        return (local_term + cross_term).astype(jnp.bfloat16)

    result = lax.map(one_block, (queries, keys_all, values_all, weights_all, stacked))
    return result.reshape(blocks_count * block_size, HEADS * HEAD_DIM)
```

```python
import functools

import jax
import jax.numpy as jnp
from jax import lax
from jax.experimental import pallas as pl
from jax.experimental.pallas import tpu as pltpu
from jax.sharding import PartitionSpec as P

CHUNKS = 4
MESH = pl.DeviceIdType.MESH
F32 = jnp.float32
BF16 = jnp.bfloat16
NT = (((1,), (1,)), ((), ()))
NN = (((1,), (0,)), ((), ()))


def kernel(dims, q_hbm, k_hbm, v_hbm, lw_hbm, out_hbm, q, k, v, lw, lam, vt, depth, own, totals,
           levels, acc, out, in_sem, out_sem, send_sem, recv_sem):
    tok, heads, width, value, bits, local_levels = dims
    half = heads // 2
    chunks = min(CHUNKS, half // 2)
    per = half // chunks
    rows = per * value
    pos = lax.axis_index("seq")
    core = pos % 2
    other = 1 - core
    last = bits - 1

    def bit(j):
        return (pos // 2 ** j) % 2

    def open_above(j):
        return (pos // 2 ** (j + 1)) != 2 ** (bits - 1 - j) - 1

    def toggled(j):
        return pos + 2 ** j * (1 - 2 * bit(j))

    relay = 2 ** (last - 1)

    barrier = pltpu.get_barrier_semaphore()
    for j in range(last):
        pl.semaphore_signal(barrier, inc=1, device_id={"seq": toggled(j)}, device_id_type=MESH)
    edge_low = (bit(last) == 0) & (bit(last - 1) == 1)
    edge_high = (bit(last) == 1) & (bit(last - 1) == 0)

    @pl.when(edge_low)
    def _():
        pl.semaphore_signal(barrier, inc=1, device_id={"seq": pos + relay}, device_id_type=MESH)

    @pl.when(edge_high)
    def _():
        pl.semaphore_signal(barrier, inc=1, device_id={"seq": pos - relay}, device_id_type=MESH)

    def cols(head, count, size):
        return pl.ds(pl.multiple_of(head * size, size * 2 if count > 1 else size), count * size)

    def first_head(side, i):
        return side * half + i * per

    order = [(other, i) for i in range(chunks)] + [(core, i) for i in range(chunks)]
    loads = []
    for n, (side, i) in enumerate(order):
        head = first_head(side, i)
        kc, vc = cols(head, per, width), cols(head, per, value)
        pair = (pltpu.make_async_copy(k_hbm.at[:, kc], k.at[:, kc], in_sem.at[2 * n]),
                pltpu.make_async_copy(v_hbm.at[:, vc], v.at[:, vc], in_sem.at[2 * n + 1]))
        for copy in pair:
            copy.start()
        loads.append(pair)
    base = 2 * len(order)
    load_q = pltpu.make_async_copy(q_hbm, q, in_sem.at[base])
    load_lw = pltpu.make_async_copy(lw_hbm, lw, in_sem.at[base + 1])
    load_q.start()
    load_lw.start()

    def state_rows(head, count=1):
        return pl.ds(pl.multiple_of(head * value, value), count * value)

    def make_state(n):
        side, i = order[n]
        for copy in loads[n]:
            copy.wait()
        head = first_head(side, i)
        for p in range(0, per, 2):
            block = v[:, cols(head + p, 2, value)]
            turned = block.astype(F32).T.astype(BF16)
            vt[state_rows(head + p, 2), :] = turned
            for s in range(2):
                own[state_rows(head + p + s), :] = lax.dot_general(
                    turned[s * value:(s + 1) * value], k[:, cols(head + p + s, 1, width)], NN,
                    preferred_element_type=F32)

    def piece(side, i):
        return state_rows(first_head(side, i), per)

    def remote(src, dst, slot, i, target):
        n = slot * chunks + i
        return pltpu.make_async_remote_copy(
            src_ref=src, dst_ref=dst, send_sem=send_sem.at[n], recv_sem=recv_sem.at[n],
            device_id={"seq": target}, device_id_type=MESH)

    mate = toggled(0)

    def swap(i):
        return remote(own.at[piece(other, i)], levels.at[0, piece(other, i)], 0, i, mate)

    def swap_in(i):
        return remote(own.at[piece(core, i)], levels.at[0, piece(core, i)], 0, i, mate)

    def extra(i):
        return remote(own.at[piece(core, i)], levels.at[0, piece(core, i)], 1, i, mate)

    def extra_in(i):
        return remote(own.at[piece(other, i)], levels.at[0, piece(other, i)], 1, i, mate)

    def main(j, i):
        target = toggled(j) if j < last else pos + relay
        return remote(totals.at[j - 1, pl.ds(i * rows, rows)], levels.at[j, piece(core, i)], 1 + j, i, target)

    def main_in(j, i):
        return remote(levels.at[j, piece(core, i)], levels.at[j, piece(core, i)], 1 + j, i, mate)

    def pass_on(i):
        return remote(levels.at[last, piece(core, i)], levels.at[last, piece(core, i)], 1 + last, i, pos + relay)

    def forward(j, i):
        return remote(levels.at[j, piece(core, i)], levels.at[j, piece(core, i)], 1 + last + j, i, mate)

    def forward_in(j, i):
        return remote(levels.at[j, piece(other, i)], levels.at[j, piece(other, i)], 1 + last + j, i, mate)

    def sends(j):
        if j == last:
            return edge_low
        up = bit(j) == 0
        return up | open_above(j) if j < last - 1 else up

    def receives(j):
        up = bit(j) == 1
        return up | open_above(j) if j < last - 1 else up

    for n in range(chunks):
        make_state(n)
        if n == 0:
            pl.semaphore_wait(barrier, last + (bit(last) + bit(last - 1)) % 2)
        swap(n).start()

    def event(j, i):
        if j == 0:
            make_state(chunks + i)

            @pl.when(core == 0)
            def _():
                extra(i).start()

            swap_in(i).wait_recv()
            mine = piece(core, i)
            totals[0, pl.ds(i * rows, rows), :] = own[mine, :] + levels[0, mine, :]

            @pl.when(sends(1))
            def _():
                main(1, i).start()
            return

        @pl.when(receives(j))
        def _():
            main_in(j, i).wait_recv()
            if j == last:
                @pl.when(edge_high)
                def _():
                    pass_on(i).start()
            else:
                @pl.when(open_above(j))
                def _():
                    part = pl.ds(i * rows, rows)
                    totals[j, part, :] = totals[j - 1, part, :] + levels[j, piece(core, i), :]

                    @pl.when(sends(j + 1))
                    def _():
                        main(j + 1, i).start()

            @pl.when(bit(j) == 1)
            def _():
                forward(j, i).start()

    def prepare():
        load_lw.wait()
        for level in range(local_levels + bits):
            lam[level] = lw[level].astype(F32)
        key_pos = lax.broadcasted_iota(jnp.int32, (tok, tok), 0)
        query_pos = lax.broadcasted_iota(jnp.int32, (tok, tok), 1)
        level_map = jnp.zeros((tok, tok), jnp.int32)
        for shift in range(local_levels - 1):
            differs = jnp.right_shift(query_pos, shift) != jnp.right_shift(key_pos, shift)
            level_map = level_map + differs.astype(jnp.int32)
        depth[...] = jnp.where(key_pos <= query_pos, level_map, local_levels)
        load_q.wait()

    def local(start, stop):
        @pl.loop(start, stop)
        def _(n):
            head = lax.rem(n + other * half, heads)
            scores = lax.dot_general(k[:, cols(head, 1, width)], q[:, cols(head, 1, width)], NT,
                                     preferred_element_type=F32)
            level_map = depth[...]
            mixing = jnp.zeros((tok, tok), F32)
            for level in range(local_levels):
                mixing = jnp.where(level_map == level, lam[level, pl.ds(head, 1), :], mixing)
            weight = (mixing * scores).astype(BF16)
            acc[state_rows(head), :] = lax.dot_general(vt[state_rows(head), :], weight, NN,
                                                       preferred_element_type=F32)

    def cross(j, side, i):
        @pl.loop(0, per)
        def _(n):
            head = first_head(side, i) + n
            part = levels[j, state_rows(head), :]
            upper = part.astype(BF16)
            lower = (part - upper.astype(F32)).astype(BF16)
            query = q[:, cols(head, 1, width)]
            product = lax.dot_general(jnp.concatenate([upper, lower], axis=1),
                                      jnp.concatenate([query, query], axis=1), NT,
                                      preferred_element_type=F32)
            acc[state_rows(head), :] += lam[local_levels + j, pl.ds(head, 1), :] * product

    def cross_level(j):
        @pl.when(bit(j) == 1)
        def _():
            for i in range(chunks):
                cross(j, core, i)
            for i in range(chunks):
                (extra_in(i) if j == 0 else forward_in(j, i)).wait_recv()
                cross(j, other, i)

    def out_copy(side, i):
        n = i if side is core else chunks + i
        part = cols(first_head(side, i), per, value)
        return pltpu.make_async_copy(out.at[:, part], out_hbm.at[:, part], out_sem.at[n])

    def finish(side, i):
        head = first_head(side, i)
        for p in range(0, per, 2):
            out[:, cols(head + p, 2, value)] = acc[state_rows(head + p, 2), :].T.astype(BF16)
        out_copy(side, i).start()

    steps = chunks + bits - 1
    share = -(-heads // (steps - 2))
    done = 0
    pending = list(range(last))
    for d in range(steps):
        for j in reversed(range(bits)):
            if 0 <= d - j < chunks:
                event(j, d - j)
        if d == 0:
            prepare()
        stop = min(heads, done + share)
        if stop > done:
            local(done, stop)
        done = stop
        if done == heads and d >= steps - last and pending:
            cross_level(pending.pop(0))
    for j in pending:
        cross_level(j)
    for side, receive in ((core, None), (other, forward_in)):
        for i in range(chunks):
            @pl.when(bit(last) == 1)
            def _():
                if receive is not None:
                    receive(last, i).wait_recv()
                cross(last, side, i)
            finish(side, i)

    for i in range(chunks):
        swap(i).wait_send()

        @pl.when(core == 0)
        def _():
            extra(i).wait_send()

        for j in range(1, bits):
            @pl.when(sends(j))
            def _():
                main(j, i).wait_send()

            @pl.when(bit(j) == 1)
            def _():
                forward(j, i).wait_send()

        @pl.when(edge_high)
        def _():
            pass_on(i).wait_send()

        out_copy(core, i).wait()
        out_copy(other, i).wait()


def on_device(query_vectors, key_vectors, value_vectors, level_weights):
    tok = query_vectors.shape[0]
    level_count, heads, _ = level_weights.shape
    width = query_vectors.shape[1] // heads
    value = value_vectors.shape[1] // heads
    bits = lax.axis_size("seq").bit_length() - 1
    local_levels = tok.bit_length()
    chunks = min(CHUNKS, heads // 4)
    slots = (1 + 2 * bits) * chunks
    anywhere = pl.BlockSpec(memory_space=pl.ANY)
    return pl.pallas_call(
        functools.partial(kernel, (tok, heads, width, value, bits, local_levels)),
        out_shape=jax.ShapeDtypeStruct((tok, heads * value), BF16),
        in_specs=[anywhere] * 4,
        out_specs=anywhere,
        scratch_shapes=[
            pltpu.VMEM(query_vectors.shape, BF16),
            pltpu.VMEM(key_vectors.shape, BF16),
            pltpu.VMEM(value_vectors.shape, BF16),
            pltpu.VMEM(level_weights.shape, BF16),
            pltpu.VMEM(level_weights.shape, F32),
            pltpu.VMEM((heads * value, tok), BF16),
            pltpu.VMEM((tok, tok), jnp.int32),
            pltpu.VMEM((heads * value, width), F32),
            pltpu.VMEM((bits - 1, heads * value // 2, width), F32),
            pltpu.VMEM((bits, heads * value, width), F32),
            pltpu.VMEM((heads * value, tok), F32),
            pltpu.VMEM((tok, heads * value), BF16),
            pltpu.SemaphoreType.DMA((4 * chunks + 2,)),
            pltpu.SemaphoreType.DMA((2 * chunks,)),
            pltpu.SemaphoreType.DMA((slots,)),
            pltpu.SemaphoreType.DMA((slots,)),
        ],
        compiler_params=pltpu.CompilerParams(collective_id=0, has_side_effects=True),
    )(query_vectors, key_vectors, value_vectors, level_weights)


def solution(mesh):
    rows = P(("grp", "seq"), None)
    placed = (rows, rows, rows, P(None, None, ("grp", "seq")))
    return jax.shard_map(on_device, mesh=mesh, in_specs=placed, out_specs=rows, check_vma=False)
```

```python
import functools

import jax
import jax.numpy as jnp
from jax import lax
from jax.experimental import pallas as pl
from jax.experimental.pallas import tpu as pltpu
from jax.sharding import PartitionSpec as P

CHUNKS = 4
GROUP = 4
MESH = pl.DeviceIdType.MESH
F32 = jnp.float32
BF16 = jnp.bfloat16
NT = (((1,), (1,)), ((), ()))
NN = (((1,), (0,)), ((), ()))


def kernel(dims, q_hbm, k_hbm, v_hbm, lw_hbm, out_hbm, q, k, v, lw, lam, vt, depth, own, totals,
           levels, acc, out, in_sem, out_sem, send_sem, recv_sem):
    tok, heads, width, value, bits, local_levels = dims
    half = heads // 2
    chunks = min(CHUNKS, half // 2)
    per = half // chunks
    rows = per * value
    pos = lax.axis_index("seq")
    core = pos % 2
    other = 1 - core
    last = bits - 1

    def bit(j):
        return (pos // 2 ** j) % 2

    def open_above(j):
        return (pos // 2 ** (j + 1)) != 2 ** (bits - 1 - j) - 1

    def toggled(j):
        return pos + 2 ** j * (1 - 2 * bit(j))

    relay = 2 ** (last - 1)

    barrier = pltpu.get_barrier_semaphore()
    for j in range(last):
        pl.semaphore_signal(barrier, inc=1, device_id={"seq": toggled(j)}, device_id_type=MESH)
    edge_low = (bit(last) == 0) & (bit(last - 1) == 1)
    edge_high = (bit(last) == 1) & (bit(last - 1) == 0)

    @pl.when(edge_low)
    def _():
        pl.semaphore_signal(barrier, inc=1, device_id={"seq": pos + relay}, device_id_type=MESH)

    @pl.when(edge_high)
    def _():
        pl.semaphore_signal(barrier, inc=1, device_id={"seq": pos - relay}, device_id_type=MESH)

    def cols(head, count, size):
        return pl.ds(pl.multiple_of(head * size, size * 2 if count > 1 else size), count * size)

    def first_head(side, i):
        return side * half + i * per

    order = [(other, i) for i in range(chunks)] + [(core, i) for i in range(chunks)]
    loads = []
    for n, (side, i) in enumerate(order):
        head = first_head(side, i)
        kc, vc = cols(head, per, width), cols(head, per, value)
        pair = (pltpu.make_async_copy(k_hbm.at[:, kc], k.at[:, kc], in_sem.at[2 * n]),
                pltpu.make_async_copy(v_hbm.at[:, vc], v.at[:, vc], in_sem.at[2 * n + 1]))
        for copy in pair:
            copy.start()
        loads.append(pair)
    base = 2 * len(order)
    load_q = pltpu.make_async_copy(q_hbm, q, in_sem.at[base])
    load_lw = pltpu.make_async_copy(lw_hbm, lw, in_sem.at[base + 1])
    load_q.start()
    load_lw.start()

    def state_rows(head, count=1):
        return pl.ds(pl.multiple_of(head * value, value), count * value)

    def make_state(n):
        side, i = order[n]
        for copy in loads[n]:
            copy.wait()
        head = first_head(side, i)
        for p in range(0, per, 2):
            block = v[:, cols(head + p, 2, value)]
            turned = block.astype(F32).T.astype(BF16)
            vt[state_rows(head + p, 2), :] = turned
            for s in range(2):
                own[state_rows(head + p + s), :] = lax.dot_general(
                    turned[s * value:(s + 1) * value], k[:, cols(head + p + s, 1, width)], NN,
                    preferred_element_type=F32)

    def piece(side, i):
        return state_rows(first_head(side, i), per)

    def remote(src, dst, slot, i, target):
        n = slot * chunks + i
        return pltpu.make_async_remote_copy(
            src_ref=src, dst_ref=dst, send_sem=send_sem.at[n], recv_sem=recv_sem.at[n],
            device_id={"seq": target}, device_id_type=MESH)

    mate = toggled(0)

    def swap(i):
        return remote(own.at[piece(other, i)], levels.at[0, piece(other, i)], 0, i, mate)

    def swap_in(i):
        return remote(own.at[piece(core, i)], levels.at[0, piece(core, i)], 0, i, mate)

    def extra(i):
        return remote(own.at[piece(core, i)], levels.at[0, piece(core, i)], 1, i, mate)

    def extra_in(i):
        return remote(own.at[piece(other, i)], levels.at[0, piece(other, i)], 1, i, mate)

    def main(j, i):
        target = toggled(j) if j < last else pos + relay
        return remote(totals.at[j - 1, pl.ds(i * rows, rows)], levels.at[j, piece(core, i)], 1 + j, i, target)

    def main_in(j, i):
        return remote(levels.at[j, piece(core, i)], levels.at[j, piece(core, i)], 1 + j, i, mate)

    def pass_on(i):
        return remote(levels.at[last, piece(core, i)], levels.at[last, piece(core, i)], 1 + last, i, pos + relay)

    def forward(j, i):
        return remote(levels.at[j, piece(core, i)], levels.at[j, piece(core, i)], 1 + last + j, i, mate)

    def forward_in(j, i):
        return remote(levels.at[j, piece(other, i)], levels.at[j, piece(other, i)], 1 + last + j, i, mate)

    def direct(i):
        return bit(last - 2) == i % 2

    def need(j, i, own_bit):
        if j == last - 1:
            return bit(last) == 0
        if j == last - 2:
            return (bit(last) == 0) | (bit(last - 1) == 0) if own_bit == i % 2 else bit(last) == 0
        return open_above(j)

    def sends(j, i):
        if j == last:
            return edge_low
        if j == last - 1:
            return (bit(j) == 0) & ((bit(last) == 0) | direct(i))
        return (bit(j) == 0) | need(j, i, 0)

    def sums(j, i):
        upper = (bit(j) == 1) & need(j, i, 1)
        return upper if j == last - 1 else upper | ((bit(j) == 0) & need(j, i, 0))

    def across(i):
        return remote(levels.at[last - 1, piece(core, i)], levels.at[last - 1, piece(core, i)],
                      2 * bits, i, toggled(last - 2))

    crossing = (bit(last) == 1) & (bit(last - 1) == 1)

    for n in range(chunks):
        make_state(n)
        if n == 0:
            pl.semaphore_wait(barrier, last + (bit(last) + bit(last - 1)) % 2)
        swap(n).start()
    for n in range(chunks):
        make_state(chunks + n)
    for i in range(chunks):
        swap_in(i).wait_recv()
        mine = piece(core, i)
        totals[0, pl.ds(i * rows, rows), :] = own[mine, :] + levels[0, mine, :]

        @pl.when(sends(1, i))
        def _():
            main(1, i).start()

    @pl.when(core == 0)
    def _():
        for i in range(chunks):
            extra(i).start()

    def event(j, i):
        if j == last - 1:
            @pl.when((bit(j) == 1) & ((bit(last) == 0) | direct(i)))
            def _():
                main_in(j, i).wait_recv()

            @pl.when(crossing & direct(i))
            def _():
                across(i).start()

            @pl.when(crossing & jnp.logical_not(direct(i)))
            def _():
                across(i).wait_recv()
        else:
            up = bit(j) == 1

            @pl.when(up if j == last else up | need(j, i, 0))
            def _():
                main_in(j, i).wait_recv()
        if j == last:
            @pl.when(edge_high)
            def _():
                pass_on(i).start()
        else:
            @pl.when(sums(j, i))
            def _():
                part = pl.ds(i * rows, rows)
                totals[j, part, :] = totals[j - 1, part, :] + levels[j, piece(core, i), :]

                @pl.when(sends(j + 1, i))
                def _():
                    main(j + 1, i).start()

        @pl.when(bit(j) == 1)
        def _():
            forward(j, i).start()

    def prepare():
        load_lw.wait()
        for level in range(local_levels + bits):
            lam[level] = lw[level].astype(F32)
        key_pos = lax.broadcasted_iota(jnp.int32, (tok, tok), 0)
        query_pos = lax.broadcasted_iota(jnp.int32, (tok, tok), 1)
        level_map = jnp.zeros((tok, tok), jnp.int32)
        for shift in range(local_levels - 1):
            differs = jnp.right_shift(query_pos, shift) != jnp.right_shift(key_pos, shift)
            level_map = level_map + differs.astype(jnp.int32)
        depth[...] = jnp.where(key_pos <= query_pos, level_map, local_levels)
        load_q.wait()

    def local(side, start, count):
        group = [side * half + start + n for n in range(count)]
        level_map = depth[...]
        scores = [lax.dot_general(k[:, cols(head, 1, width)], q[:, cols(head, 1, width)], NT,
                                  preferred_element_type=F32) for head in group]
        values = [vt[state_rows(head), :] for head in group]
        weights = []
        for n, head in enumerate(group):
            mixing = jnp.zeros((tok, tok), F32)
            for level in range(local_levels):
                mixing = jnp.where(level_map == level, lam[level, pl.ds(head, 1), :], mixing)
            weights.append((mixing * scores[n]).astype(BF16))
        results = [lax.dot_general(value_rows, weight, NN, preferred_element_type=F32)
                   for value_rows, weight in zip(values, weights)]
        for head, result in zip(group, results):
            acc[state_rows(head), :] = result

    def cross(j, side, i):
        group = [first_head(side, i) + n for n in range(per)]
        pairs = []
        for head in group:
            part = levels[j, state_rows(head), :]
            upper = part.astype(BF16)
            lower = (part - upper.astype(F32)).astype(BF16)
            pairs.append(jnp.concatenate([upper, lower], axis=1))
        queries = [q[:, cols(head, 1, width)] for head in group]
        products = [lax.dot_general(pair, jnp.concatenate([query, query], axis=1), NT,
                                    preferred_element_type=F32) for pair, query in zip(pairs, queries)]
        results = [acc[state_rows(head), :] + lam[local_levels + j, pl.ds(head, 1), :] * product
                   for head, product in zip(group, products)]
        for head, result in zip(group, results):
            acc[state_rows(head), :] = result

    def cross_piece(j, side, i):
        @pl.when(bit(j) == 1)
        def _():
            if side is other:
                (extra_in(i) if j == 0 else forward_in(j, i)).wait_recv()
            cross(j, side, i)

    def out_copy(side, i):
        n = i if side is core else chunks + i
        part = cols(first_head(side, i), per, value)
        return pltpu.make_async_copy(out.at[:, part], out_hbm.at[:, part], out_sem.at[n])

    def finish(side, i):
        head = first_head(side, i)
        for p in range(0, per, 2):
            out[:, cols(head + p, 2, value)] = acc[state_rows(head + p, 2), :].T.astype(BF16)
        out_copy(side, i).start()

    prepare()
    events = sorted(((j, i) for j in range(1, bits) for i in range(chunks)), key=lambda e: (e[0] + e[1], e[0]))
    at = {e: n for n, e in enumerate(events)}
    group = min(GROUP, half)
    work = [(-1, 2, functools.partial(local, side, start, group))
            for side in (other, core) for start in range(0, half, group)]
    for j in range(last):
        for side in (core, other):
            for i in range(chunks):
                ready = at[j, min(i + (side is other), chunks - 1)] if j else -1
                work.append((ready, 1 / chunks * 4, functools.partial(cross_piece, j, side, i)))
    budget = sum(w[1] for w in work) / (len(events) - 1)
    spent = 0.0

    def spend(n, limit):
        nonlocal spent
        while work and work[0][0] <= n and spent < limit:
            _, weight, run = work.pop(0)
            run()
            spent += weight

    spend(-1, budget)
    for n, e in enumerate(events):
        event(*e)
        spend(n, budget * (n + 2))
    spend(len(events), float("inf"))
    for i in range(chunks):
        cross_piece(last, core, i)
        finish(core, i)
        cross_piece(last, other, i)
        finish(other, i)

    for i in range(chunks):
        swap(i).wait_send()

        @pl.when(core == 0)
        def _():
            extra(i).wait_send()

        for j in range(1, bits):
            @pl.when(sends(j, i))
            def _():
                main(j, i).wait_send()

            @pl.when(bit(j) == 1)
            def _():
                forward(j, i).wait_send()

        @pl.when(edge_high)
        def _():
            pass_on(i).wait_send()

        @pl.when(crossing & direct(i))
        def _():
            across(i).wait_send()

        out_copy(core, i).wait()
        out_copy(other, i).wait()


def on_device(query_vectors, key_vectors, value_vectors, level_weights):
    tok = query_vectors.shape[0]
    level_count, heads, _ = level_weights.shape
    width = query_vectors.shape[1] // heads
    value = value_vectors.shape[1] // heads
    bits = lax.axis_size("seq").bit_length() - 1
    local_levels = tok.bit_length()
    chunks = min(CHUNKS, heads // 4)
    slots = (1 + 2 * bits) * chunks
    anywhere = pl.BlockSpec(memory_space=pl.ANY)
    return pl.pallas_call(
        functools.partial(kernel, (tok, heads, width, value, bits, local_levels)),
        out_shape=jax.ShapeDtypeStruct((tok, heads * value), BF16),
        in_specs=[anywhere] * 4,
        out_specs=anywhere,
        scratch_shapes=[
            pltpu.VMEM(query_vectors.shape, BF16),
            pltpu.VMEM(key_vectors.shape, BF16),
            pltpu.VMEM(value_vectors.shape, BF16),
            pltpu.VMEM(level_weights.shape, BF16),
            pltpu.VMEM(level_weights.shape, F32),
            pltpu.VMEM((heads * value, tok), BF16),
            pltpu.VMEM((tok, tok), jnp.int32),
            pltpu.VMEM((heads * value, width), F32),
            pltpu.VMEM((bits - 1, heads * value // 2, width), F32),
            pltpu.VMEM((bits, heads * value, width), F32),
            pltpu.VMEM((heads * value, tok), F32),
            pltpu.VMEM((tok, heads * value), BF16),
            pltpu.SemaphoreType.DMA((4 * chunks + 2,)),
            pltpu.SemaphoreType.DMA((2 * chunks,)),
            pltpu.SemaphoreType.DMA((slots,)),
            pltpu.SemaphoreType.DMA((slots,)),
        ],
        compiler_params=pltpu.CompilerParams(collective_id=0, has_side_effects=True),
    )(query_vectors, key_vectors, value_vectors, level_weights)


def solution(mesh):
    rows = P(("grp", "seq"), None)
    placed = (rows, rows, rows, P(None, None, ("grp", "seq")))
    return jax.shard_map(on_device, mesh=mesh, in_specs=placed, out_specs=rows, check_vma=False)
```

```python
import functools

import jax
import jax.numpy as jnp
from jax import lax
from jax.experimental import pallas as pl
from jax.experimental.pallas import tpu as pltpu
from jax.sharding import PartitionSpec as P

CHUNKS = 4
GROUP = 4
MESH = pl.DeviceIdType.MESH
F32 = jnp.float32
BF16 = jnp.bfloat16
NT = (((1,), (1,)), ((), ()))
NN = (((1,), (0,)), ((), ()))


def kernel(dims, q_hbm, k_hbm, v_hbm, lw_hbm, out_hbm, q, k, v, lw, lam, vt, depth, own, totals,
           levels, acc, out, in_sem, out_sem, send_sem, recv_sem):
    tok, heads, width, value, bits, local_levels = dims
    half = heads // 2
    chunks = min(CHUNKS, half // 2)
    per = half // chunks
    rows = per * value
    pos = lax.axis_index("seq")
    core = pos % 2
    other = 1 - core
    last = bits - 1

    def bit(j):
        return (pos // 2 ** j) % 2

    def open_above(j):
        return (pos // 2 ** (j + 1)) != 2 ** (bits - 1 - j) - 1

    def toggled(j):
        return pos + 2 ** j * (1 - 2 * bit(j))

    relay = 2 ** (last - 1)

    barrier = pltpu.get_barrier_semaphore()
    for j in range(last):
        pl.semaphore_signal(barrier, inc=1, device_id={"seq": toggled(j)}, device_id_type=MESH)
    edge_low = (bit(last) == 0) & (bit(last - 1) == 1)
    edge_high = (bit(last) == 1) & (bit(last - 1) == 0)

    @pl.when(edge_low)
    def _():
        pl.semaphore_signal(barrier, inc=1, device_id={"seq": pos + relay}, device_id_type=MESH)

    @pl.when(edge_high)
    def _():
        pl.semaphore_signal(barrier, inc=1, device_id={"seq": pos - relay}, device_id_type=MESH)

    def cols(head, count, size):
        return pl.ds(pl.multiple_of(head * size, size * 2 if count > 1 else size), count * size)

    def first_head(side, i):
        return side * half + i * per

    order = [(other, i) for i in range(chunks)] + [(core, i) for i in range(chunks)]
    loads = []
    for n, (side, i) in enumerate(order):
        head = first_head(side, i)
        kc, vc = cols(head, per, width), cols(head, per, value)
        pair = (pltpu.make_async_copy(k_hbm.at[:, kc], k.at[:, kc], in_sem.at[2 * n]),
                pltpu.make_async_copy(v_hbm.at[:, vc], v.at[:, vc], in_sem.at[2 * n + 1]))
        for copy in pair:
            copy.start()
        loads.append(pair)
    base = 2 * len(order)
    load_q = pltpu.make_async_copy(q_hbm, q, in_sem.at[base])
    load_lw = pltpu.make_async_copy(lw_hbm, lw, in_sem.at[base + 1])
    load_q.start()
    load_lw.start()

    def state_rows(head, count=1):
        return pl.ds(pl.multiple_of(head * value, value), count * value)

    def make_state(n):
        side, i = order[n]
        for copy in loads[n]:
            copy.wait()
        head = first_head(side, i)
        for p in range(0, per, 2):
            block = v[:, cols(head + p, 2, value)]
            turned = block.astype(F32).T.astype(BF16)
            vt[state_rows(head + p, 2), :] = turned
            for s in range(2):
                own[state_rows(head + p + s), :] = lax.dot_general(
                    turned[s * value:(s + 1) * value], k[:, cols(head + p + s, 1, width)], NN,
                    preferred_element_type=F32)

    def piece(side, i):
        return state_rows(first_head(side, i), per)

    def remote(src, dst, slot, i, target):
        n = slot * chunks + i
        return pltpu.make_async_remote_copy(
            src_ref=src, dst_ref=dst, send_sem=send_sem.at[n], recv_sem=recv_sem.at[n],
            device_id={"seq": target}, device_id_type=MESH)

    mate = toggled(0)

    def swap(i):
        return remote(own.at[piece(other, i)], levels.at[0, piece(other, i)], 0, i, mate)

    def swap_in(i):
        return remote(own.at[piece(core, i)], levels.at[0, piece(core, i)], 0, i, mate)

    def extra(i):
        return remote(own.at[piece(core, i)], levels.at[0, piece(core, i)], 1, i, mate)

    def extra_in(i):
        return remote(own.at[piece(other, i)], levels.at[0, piece(other, i)], 1, i, mate)

    def main(j, i):
        target = toggled(j) if j < last else pos + relay
        return remote(totals.at[j - 1, pl.ds(i * rows, rows)], levels.at[j, piece(core, i)], 1 + j, i, target)

    def main_in(j, i):
        return remote(levels.at[j, piece(core, i)], levels.at[j, piece(core, i)], 1 + j, i, mate)

    def pass_on(i):
        return remote(levels.at[last, piece(core, i)], levels.at[last, piece(core, i)], 1 + last, i, pos + relay)

    def forward(j, i):
        return remote(levels.at[j, piece(core, i)], levels.at[j, piece(core, i)], 1 + last + j, i, mate)

    def forward_in(j, i):
        return remote(levels.at[j, piece(other, i)], levels.at[j, piece(other, i)], 1 + last + j, i, mate)

    def direct(i):
        return bit(last - 2) == i % 2

    def need(j, i, own_bit):
        if j == last - 1:
            return bit(last) == 0
        if j == last - 2:
            return (bit(last) == 0) | (bit(last - 1) == 0) if own_bit == i % 2 else bit(last) == 0
        return open_above(j)

    def sends(j, i):
        if j == last:
            return edge_low
        if j == last - 1:
            return (bit(j) == 0) & ((bit(last) == 0) | direct(i))
        return (bit(j) == 0) | need(j, i, 0)

    def sums(j, i):
        upper = (bit(j) == 1) & need(j, i, 1)
        return upper if j == last - 1 else upper | ((bit(j) == 0) & need(j, i, 0))

    def across(i):
        return remote(levels.at[last - 1, piece(core, i)], levels.at[last - 1, piece(core, i)],
                      2 * bits, i, toggled(last - 2))

    crossing = (bit(last) == 1) & (bit(last - 1) == 1)

    for n in range(chunks):
        make_state(n)
        if n == 0:
            pl.semaphore_wait(barrier, last + (bit(last) + bit(last - 1)) % 2)
        swap(n).start()
    for n in range(chunks):
        make_state(chunks + n)
    for i in range(chunks):
        swap_in(i).wait_recv()
        mine = piece(core, i)
        totals[0, pl.ds(i * rows, rows), :] = own[mine, :] + levels[0, mine, :]

        @pl.when(sends(1, i))
        def _():
            main(1, i).start()

    @pl.when(core == 0)
    def _():
        for i in range(chunks):
            extra(i).start()

    def event(j, i):
        if j == last - 1:
            @pl.when((bit(j) == 1) & ((bit(last) == 0) | direct(i)))
            def _():
                main_in(j, i).wait_recv()

            @pl.when(crossing & direct(i))
            def _():
                across(i).start()

            @pl.when(crossing & jnp.logical_not(direct(i)))
            def _():
                across(i).wait_recv()
        else:
            up = bit(j) == 1

            @pl.when(up if j == last else up | need(j, i, 0))
            def _():
                main_in(j, i).wait_recv()
        if j == last:
            @pl.when(edge_high)
            def _():
                pass_on(i).start()
        else:
            @pl.when(sums(j, i))
            def _():
                part = pl.ds(i * rows, rows)
                totals[j, part, :] = totals[j - 1, part, :] + levels[j, piece(core, i), :]

                @pl.when(sends(j + 1, i))
                def _():
                    main(j + 1, i).start()

        @pl.when(bit(j) == 1)
        def _():
            forward(j, i).start()

    def prepare():
        load_lw.wait()
        for level in range(local_levels + bits):
            lam[level] = lw[level].astype(F32)
        key_pos = lax.broadcasted_iota(jnp.int32, (tok, tok), 0)
        query_pos = lax.broadcasted_iota(jnp.int32, (tok, tok), 1)
        level_map = jnp.zeros((tok, tok), jnp.int32)
        for shift in range(local_levels - 1):
            differs = jnp.right_shift(query_pos, shift) != jnp.right_shift(key_pos, shift)
            level_map = level_map + differs.astype(jnp.int32)
        depth[...] = jnp.where(key_pos <= query_pos, level_map, local_levels)
        load_q.wait()

    def local(side, start, count):
        group = [side * half + start + n for n in range(count)]
        level_map = depth[...]
        scores = [lax.dot_general(k[:, cols(head, 1, width)], q[:, cols(head, 1, width)], NT,
                                  preferred_element_type=F32) for head in group]
        values = [vt[state_rows(head), :] for head in group]
        weights = []
        for n, head in enumerate(group):
            mixing = jnp.zeros((tok, tok), F32)
            for level in range(local_levels):
                mixing = jnp.where(level_map == level, lam[level, pl.ds(head, 1), :], mixing)
            weights.append((mixing * scores[n]).astype(BF16))
        results = [lax.dot_general(value_rows, weight, NN, preferred_element_type=F32)
                   for value_rows, weight in zip(values, weights)]
        for head, result in zip(group, results):
            acc[state_rows(head), :] = result

    def cross(j, side, i):
        group = [first_head(side, i) + n for n in range(per)]
        pairs = []
        for head in group:
            part = levels[j, state_rows(head), :]
            upper = part.astype(BF16)
            lower = (part - upper.astype(F32)).astype(BF16)
            pairs.append(jnp.concatenate([upper, lower], axis=1))
        queries = [q[:, cols(head, 1, width)] for head in group]
        products = [lax.dot_general(pair, jnp.concatenate([query, query], axis=1), NT,
                                    preferred_element_type=F32) for pair, query in zip(pairs, queries)]
        results = [acc[state_rows(head), :] + lam[local_levels + j, pl.ds(head, 1), :] * product
                   for head, product in zip(group, products)]
        for head, result in zip(group, results):
            acc[state_rows(head), :] = result

    def cross_piece(j, side, i):
        @pl.when(bit(j) == 1)
        def _():
            if side is other:
                (extra_in(i) if j == 0 else forward_in(j, i)).wait_recv()
            cross(j, side, i)

    def out_copy(side, i):
        n = i if side is core else chunks + i
        part = cols(first_head(side, i), per, value)
        return pltpu.make_async_copy(out.at[:, part], out_hbm.at[:, part], out_sem.at[n])

    def finish(side, i):
        head = first_head(side, i)
        for p in range(0, per, 2):
            out[:, cols(head + p, 2, value)] = acc[state_rows(head + p, 2), :].T.astype(BF16)
        out_copy(side, i).start()

    prepare()
    events = sorted(((j, i) for j in range(1, bits) for i in range(chunks)), key=lambda e: (e[0] + e[1], e[0]))
    at = {e: n for n, e in enumerate(events)}
    group = min(GROUP, half)
    work = [(-1, 2, functools.partial(local, side, start, group))
            for side in (other, core) for start in range(0, half, group)]
    for j in range(last):
        for side in (core, other):
            for i in range(chunks):
                ready = at[j, min(i + (side is other), chunks - 1)] if j else -1
                work.append((ready, 1 / chunks * 4, functools.partial(cross_piece, j, side, i)))
    def close(side, i):
        cross_piece(last, side, i)
        finish(side, i)

    ends = [(at[last, min(i + (side is other), chunks - 1)], 0, functools.partial(close, side, i))
            for i in range(chunks) for side in (core, other)]
    work += sorted(ends, key=lambda w: w[0])
    budget = sum(w[1] for w in work) / (len(events) - 1)
    spent = 0.0

    def spend(n, limit):
        nonlocal spent
        while work and work[0][0] <= n and spent < limit:
            _, weight, run = work.pop(0)
            run()
            spent += weight

    spend(-1, budget)
    for n, e in enumerate(events):
        event(*e)
        spend(n, budget * (n + 2))
    spend(len(events), float("inf"))
    for i in range(chunks):
        swap(i).wait_send()

        @pl.when(core == 0)
        def _():
            extra(i).wait_send()

        for j in range(1, bits):
            @pl.when(sends(j, i))
            def _():
                main(j, i).wait_send()

            @pl.when(bit(j) == 1)
            def _():
                forward(j, i).wait_send()

        @pl.when(edge_high)
        def _():
            pass_on(i).wait_send()

        @pl.when(crossing & direct(i))
        def _():
            across(i).wait_send()

        out_copy(core, i).wait()
        out_copy(other, i).wait()


def on_device(query_vectors, key_vectors, value_vectors, level_weights):
    tok = query_vectors.shape[0]
    level_count, heads, _ = level_weights.shape
    width = query_vectors.shape[1] // heads
    value = value_vectors.shape[1] // heads
    bits = lax.axis_size("seq").bit_length() - 1
    local_levels = tok.bit_length()
    chunks = min(CHUNKS, heads // 4)
    slots = (1 + 2 * bits) * chunks
    anywhere = pl.BlockSpec(memory_space=pl.ANY)
    return pl.pallas_call(
        functools.partial(kernel, (tok, heads, width, value, bits, local_levels)),
        out_shape=jax.ShapeDtypeStruct((tok, heads * value), BF16),
        in_specs=[anywhere] * 4,
        out_specs=anywhere,
        scratch_shapes=[
            pltpu.VMEM(query_vectors.shape, BF16),
            pltpu.VMEM(key_vectors.shape, BF16),
            pltpu.VMEM(value_vectors.shape, BF16),
            pltpu.VMEM(level_weights.shape, BF16),
            pltpu.VMEM(level_weights.shape, F32),
            pltpu.VMEM((heads * value, tok), BF16),
            pltpu.VMEM((tok, tok), jnp.int32),
            pltpu.VMEM((heads * value, width), F32),
            pltpu.VMEM((bits - 1, heads * value // 2, width), F32),
            pltpu.VMEM((bits, heads * value, width), F32),
            pltpu.VMEM((heads * value, tok), F32),
            pltpu.VMEM((tok, heads * value), BF16),
            pltpu.SemaphoreType.DMA((4 * chunks + 2,)),
            pltpu.SemaphoreType.DMA((2 * chunks,)),
            pltpu.SemaphoreType.DMA((slots,)),
            pltpu.SemaphoreType.DMA((slots,)),
        ],
        compiler_params=pltpu.CompilerParams(collective_id=0, has_side_effects=True),
    )(query_vectors, key_vectors, value_vectors, level_weights)


def solution(mesh):
    rows = P(("grp", "seq"), None)
    placed = (rows, rows, rows, P(None, None, ("grp", "seq")))
    return jax.shard_map(on_device, mesh=mesh, in_specs=placed, out_specs=rows, check_vma=False)
```
